32 devices in a mesh: dp: 4 (over z), mp: 8 (over y, x, core).
Axes of the slice: x: 2, y: 2, z: 4, core: 2. Of those that a mesh axis runs over, the one named last changes fastest.
Arguments:
- tokens: bfloat16 [4096, 4096], P(('dp', 'mp')), may hold values from -6 to 6
- expert_ids: int32 [4096, 1], P(('dp', 'mp')), may hold values from 0 to 15; in each aligned block of 128 rows (0 to 127, 128 to 255, ...) at most 12 rows name the same one
- gate_probs: float32 [4096, 1], P(('dp', 'mp')), may hold values from 0.3 to 1
- gate_weight: bfloat16 [16, 4096, 1536], P('mp', None, 'dp'), may hold values from -0.09375 to 0.09375
- up_weight: bfloat16 [16, 4096, 1536], P('mp', None, 'dp'), may hold values from -0.09375 to 0.09375
- down_weight: bfloat16 [16, 1536, 4096], P('mp', 'dp'), may hold values from -0.15625 to 0.15625
- sign_offset: int32 [1], replicated, may hold values from 1 to 999999999
Outputs:
- out_plus: bfloat16 [4096, 4096], P(('dp', 'mp'))
- out_minus: bfloat16 [4096, 4096], P(('dp', 'mp'))
The draws below stay inside these ranges and needn't reach their ends.
Inputs may be any that keep to these rules, and one draw needn't show every extreme that they name: `expert_ids`: within each aligned block of 128 tokens (the tokens of one device) no expert is named by more than 12 routes, a bound that some block reaches.
All inputs are finite; a program needn't handle non-finite values.
Results may differ from the reference program's by a relative error of at most 0.01.
Values may be sent and summed in bfloat16 or wider, within the bound.
No kernel may reach another device: no remote copies, remote signals or barrier semaphores. Data moves between devices by JAX's collectives and lax.ppermute only.
A program may use at most 128 MiB of HBM per device.

```python
import math
import jax
import jax.numpy as jnp
import numpy as np
from jax import lax

D = 4096
FF = 1536
TOP = 1
TOK_DEV = 128
EXPERTS = 16
TOKENS = 4096
CAP = 12
N_DP = 4


def level_of(key, shape, shards, least, largest):
    gain, own = 1.0, jax.random.fold_in(key, 6)
    for axis_at, parts in shards:
        draws = jnp.exp(jax.random.uniform(jax.random.fold_in(own, axis_at), (parts,), jnp.float32, least / len(shards), largest / len(shards)))
        gain = gain * jnp.repeat(draws, shape[axis_at] // parts).reshape([-1 if axis == axis_at else 1 for axis in range(len(shape))])
    return gain


def routed_block(rng, own, number, rows, number_of, top, most, skew):
    ranking = jax.random.permutation(rng, number_of)
    packed, usual = portions_of(number_of, rows * top, most, skew, True), portions_of(number_of, rows * top, most, skew, False)
    places = jnp.arange(number_of)

    def named(tallies, turn):
        used = int((tallies > 0).sum())
        fixed = max(1, used // 4)
        shifted = fixed + (places - fixed + turn * (used - fixed)) % max(1, number_of - fixed)
        return jnp.zeros((number_of,), jnp.int32).at[ranking[jnp.where(places < fixed, places, shifted)]].set(jnp.asarray(tallies, jnp.int32))

    tallies = jnp.where(number % 4 == 0, named(packed, number // 4), named(usual, number - number // 4 - 1))
    mixed = jax.random.permutation(jax.random.fold_in(own, 3), number_of)
    donor, receiver = mixed[0:number_of // 2 * 2:2], mixed[1:number_of // 2 * 2:2]
    room = jnp.minimum(tallies[donor] - 1, most - tallies[receiver]) // 2
    room = jnp.where((donor == ranking[0]) | (receiver == ranking[0]) | (tallies[receiver] == 0), 0, jnp.maximum(room, 0))
    shifted = jax.random.randint(jax.random.fold_in(own, 4), (number_of // 2,), 0, 1 << 20) % (room + 1)
    tallies = tallies.at[donor].add(-shifted).at[receiver].add(shifted)
    members = jnp.searchsorted(jnp.cumsum(tallies), jnp.arange(rows * top), side="right").astype(jnp.int32)
    grid = members.reshape(top, rows).T
    grid = grid[jax.random.permutation(jax.random.fold_in(own, 1), rows)]
    turn = jax.random.randint(jax.random.fold_in(own, 2), (rows, 1), 0, top)
    return jnp.take_along_axis(grid, (jnp.arange(top)[None, :] + turn) % top, axis=1)


def portions_of(count, total, most, skew, full):
    loads = [(1 << 20) // math.isqrt(standing ** skew) + 1 for standing in range(1, count + 1)]
    largest = most if full else min(most, max(-(-total // count), total * loads[0] // sum(loads)))
    least = 1 if total - largest >= count - 1 else 0
    counts, rest = [largest] + [least] * (count - 1), total - largest - least * (count - 1)
    while rest > 0:
        candidates = [i for i in range(1, count) if counts[i] < largest] or [i for i in range(1, count) if counts[i] < most]
        mass, left = sum([loads[i] for i in candidates]), rest
        for i in candidates:
            addition = min(most - counts[i], max(1, left * loads[i] // mass), rest)
            counts[i] = counts[i] + addition
            rest = rest - addition
    return np.array(counts)


def scatter_about(stream_key, dims, spread, bound, pieces=(), kind=jnp.bfloat16):
    drawn = jax.random.normal(stream_key, dims, jnp.float32) * spread
    if len(pieces) > 0:
        drawn = level_of(stream_key, dims, pieces, -0.22, 0.18) * drawn
    return jnp.clip(drawn, min=-bound, max=bound).astype(kind)


def setup_inputs(seed: int = 0) -> dict:
    seeds = jax.random.split(jax.random.key(seed), 8)
    tokens = scatter_about(seeds[0], (TOKENS, D), 1.0, 6.0, ((0, 32),))
    expert_ids_keys = jax.random.split(jax.random.fold_in(seeds[1], 1), TOKENS // TOK_DEV)
    expert_ids_turns = jax.random.permutation(jax.random.fold_in(seeds[1], 3), TOKENS // TOK_DEV)
    expert_ids = jax.vmap(lambda own, number: routed_block(jax.random.fold_in(seeds[1], 2), own, number, TOK_DEV, EXPERTS, TOP, CAP, 2))(expert_ids_keys, expert_ids_turns).reshape((TOKENS, TOP))
    gate_probs = jnp.clip(0.3 + 0.7 * jax.random.uniform(seeds[2], (TOKENS, TOP), jnp.float32) ** level_of(seeds[2], (TOKENS, TOP), ((0, 32),), -0.2, 0.2), 0.3, 1.0)
    gate_weight = scatter_about(seeds[3], (EXPERTS, D, FF), D ** -0.5, 0.09375, ((0, 8), (2, 4)))
    up_weight = scatter_about(seeds[4], (EXPERTS, D, FF), D ** -0.5, 0.09375, ((0, 8), (2, 4)))
    down_weight = scatter_about(seeds[5], (EXPERTS, FF, D), FF ** -0.5, 0.15625, ((0, 8), (1, 4)))
    sign_offset = jax.random.randint(seeds[6], (1,), 1, 1000000000).astype(jnp.int32)
    return {"tokens": tokens, "expert_ids": expert_ids, "gate_probs": gate_probs, "gate_weight": gate_weight, "up_weight": up_weight, "down_weight": down_weight, "sign_offset": sign_offset}


epsilon_step = 0.005


def mixing(number):
    number = number ^ lax.shift_right_logical(number, jnp.full_like(number, 16))
    number = number * 73244475
    number = number ^ lax.shift_right_logical(number, jnp.full_like(number, 16))
    number = number * 73244475
    return number ^ lax.shift_right_logical(number, jnp.full_like(number, 16))


def sign_noise(offset_mixed, position, matrix_tag):
    hashed = mixing((position * 3 + matrix_tag) ^ offset_mixed)
    parity = lax.shift_right_logical(hashed, jnp.full_like(hashed, 9)) & 1
    return (parity * 2 - 1).astype(jnp.float32)


def perturb(weight, noise, direction):
    return (weight.astype(jnp.float32) + direction * epsilon_step * noise).astype(jnp.bfloat16)


def reference(tokens, expert_ids, gate_probs, gate_weight, up_weight, down_weight, sign_offset):
    blocks = TOKENS // TOK_DEV
    per_block = TOK_DEV * TOP
    offset_mixed = mixing(sign_offset[0] * 668265261 + 12345)
    routes = expert_ids.reshape(blocks, per_block)
    expert_axis = jnp.arange(EXPERTS, dtype=jnp.int32)
    onehot = (routes[:, :, None] == expert_axis[None, None, :]).astype(jnp.int32)
    earlier = (jnp.cumsum(onehot, axis=1, dtype=jnp.int32) - onehot).astype(jnp.int32)
    rank_in = jnp.sum(earlier * onehot, axis=2, dtype=jnp.int32).astype(jnp.int32)
    block_axis = jnp.arange(blocks, dtype=jnp.int32)
    column = (routes * (blocks * CAP) + block_axis[:, None] * CAP + rank_in).reshape(-1).astype(jnp.int32)
    repeated = jnp.repeat(tokens, TOP, axis=0)
    buffer = jnp.zeros((EXPERTS * blocks * CAP, D), jnp.bfloat16).at[column].set(repeated)
    buffer = buffer.reshape(EXPERTS, blocks * CAP, D)
    width_axis = jnp.arange(D, dtype=jnp.int32)
    unit_axis = jnp.arange(FF, dtype=jnp.int32)
    quarter = FF // N_DP

    def one_expert(inputs):
        row_block, gate_one, up_one, down_one, expert = inputs
        gate_pos = (expert * D + width_axis[:, None]) * FF + unit_axis[None, :]
        down_pos = (expert * FF + unit_axis[:, None]) * D + width_axis[None, :]
        noise_gate = sign_noise(offset_mixed, gate_pos, 0)
        noise_up = sign_noise(offset_mixed, gate_pos, 1)
        noise_down = sign_noise(offset_mixed, down_pos, 2)
        results = []
        for direction in (1.0, -1.0):
            gate_moved = perturb(gate_one, noise_gate, direction)
            up_moved = perturb(up_one, noise_up, direction)
            down_moved = perturb(down_one, noise_down, direction)
            gate_act = jnp.dot(row_block, gate_moved, preferred_element_type=jnp.float32)
            up_act = jnp.dot(row_block, up_moved, preferred_element_type=jnp.float32)
            hidden = (jax.nn.silu(gate_act) * up_act).astype(jnp.bfloat16)
            running = jnp.zeros((row_block.shape[0], D), jnp.float32)
            for part_index in range(N_DP):
                first_unit = part_index * quarter
                partial_value = jnp.dot(hidden[:, first_unit:first_unit + quarter], down_moved[first_unit:first_unit + quarter], preferred_element_type=jnp.float32).astype(jnp.bfloat16)
                running = running + lax.optimization_barrier(partial_value).astype(jnp.float32)
            results.append(running.astype(jnp.bfloat16))
        return jnp.stack(results, axis=1)

    outputs = lax.map(one_expert, (buffer, gate_weight, up_weight, down_weight, expert_axis))
    flat_out = outputs.reshape(EXPERTS * blocks * CAP, 2, D)
    picked = jnp.take(flat_out, column, axis=0).reshape(TOKENS, TOP, 2, D).astype(jnp.float32)
    weighted = jnp.sum(gate_probs[:, :, None, None] * picked, axis=1)
    return weighted[:, 0].astype(jnp.bfloat16), weighted[:, 1].astype(jnp.bfloat16)
```

```python
import functools

import jax
import jax.numpy as jnp
from jax import lax
from jax.experimental import pallas as pl
from jax.experimental.pallas import tpu as pltpu
from jax.sharding import PartitionSpec as P

EPSILON = 0.005
MULTIPLIER = 73244475


def logical_right(number, amount):
    return lax.shift_right_logical(number, jnp.full_like(number, amount))


def mixing(number):
    number = number ^ logical_right(number, 16)
    number = number * MULTIPLIER
    number = number ^ logical_right(number, 16)
    number = number * MULTIPLIER
    return number ^ logical_right(number, 16)


def signed_step(hashed):
    hashed = hashed ^ logical_right(hashed, 16)
    hashed = hashed * MULTIPLIER
    hashed = hashed ^ logical_right(hashed, 16)
    hashed = hashed * MULTIPLIER
    bit = (hashed ^ logical_right(hashed, 16)) & 512
    return jnp.where(bit != 0, jnp.float32(EPSILON), jnp.float32(-EPSILON))


def cost(flops, moved):
    return pl.CostEstimate(flops=int(flops), bytes_accessed=int(moved), transcendentals=0)


SMEM_SPEC = pl.BlockSpec(memory_space=pltpu.SMEM)


def perturb_gate_up(params, gate, up, hidden_total):
    local, width, quarter = gate.shape
    step_rows = min(256, width)

    def body(params_ref, gate_ref, up_ref, plus_ref, minus_ref, lin_ref):
        step = pl.program_id(0)

        @pl.when(step == 0)
        def _():
            row = lax.broadcasted_iota(jnp.int32, lin_ref.shape, 0)
            col = lax.broadcasted_iota(jnp.int32, lin_ref.shape, 1)
            lin_ref[...] = (row * hidden_total + col) * 3

        for expert in range(local):
            first = ((params_ref[1] + expert) * width + step * step_rows) * hidden_total + params_ref[2]
            for tag, source in ((0, gate_ref), (1, up_ref)):
                delta = signed_step((lin_ref[...] + (first * 3 + tag)) ^ params_ref[0])
                weight = source[expert].astype(jnp.float32)
                columns = pl.ds((expert * 2 + tag) * quarter, quarter)
                plus_ref[:, columns] = (weight + delta).astype(jnp.bfloat16)
                minus_ref[:, columns] = (weight - delta).astype(jnp.bfloat16)

    shape = jax.ShapeDtypeStruct((width, local * 2 * quarter), jnp.bfloat16)
    out_spec = pl.BlockSpec((step_rows, local * 2 * quarter), lambda i: (i, 0))
    in_spec = pl.BlockSpec((local, step_rows, quarter), lambda i: (0, i, 0))
    return pl.pallas_call(
        body,
        grid=(width // step_rows,),
        in_specs=[SMEM_SPEC, in_spec, in_spec],
        out_specs=[out_spec, out_spec],
        out_shape=[shape, shape],
        scratch_shapes=[pltpu.VMEM((step_rows, quarter), jnp.int32)],
        cost_estimate=cost(0, gate.size * 12),
        name="perturb_gate_up",
    )(params, gate, up)


def perturb_down(params, down, hidden_total):
    local, quarter, width = down.shape
    step_rows = 64 if quarter % 64 == 0 else quarter
    per_expert = quarter // step_rows

    def body(params_ref, down_ref, plus_ref, minus_ref, lin_ref):
        step = pl.program_id(0)

        @pl.when(step == 0)
        def _():
            row = lax.broadcasted_iota(jnp.int32, lin_ref.shape, 0)
            col = lax.broadcasted_iota(jnp.int32, lin_ref.shape, 1)
            lin_ref[...] = (row * width + col) * 3

        expert = step // per_expert
        first = (params_ref[1] + expert) * hidden_total + params_ref[2] + (step % per_expert) * step_rows
        delta = signed_step((lin_ref[...] + (first * width * 3 + 2)) ^ params_ref[0])
        weight = down_ref[...].astype(jnp.float32)
        plus_ref[...] = (weight + delta).astype(jnp.bfloat16)
        minus_ref[...] = (weight - delta).astype(jnp.bfloat16)

    shape = jax.ShapeDtypeStruct((local * quarter, width), jnp.bfloat16)
    spec = pl.BlockSpec((step_rows, width), lambda i: (i, 0))
    return pl.pallas_call(
        body,
        grid=(local * per_expert,),
        in_specs=[SMEM_SPEC, spec],
        out_specs=[spec, spec],
        out_shape=[shape, shape],
        scratch_shapes=[pltpu.VMEM((step_rows, width), jnp.int32)],
        cost_estimate=cost(0, down.size * 6),
        name="perturb_down",
    )(params, down.reshape(local * quarter, width))


def selector(ids, me, local, capacity, slots_total):
    count = ids.shape[1]
    across = jnp.broadcast_to(ids, (count, count))
    down = jnp.transpose(across.astype(jnp.float32)).astype(jnp.int32)
    earlier = lax.broadcasted_iota(jnp.int32, (count, count), 0) < lax.broadcasted_iota(
        jnp.int32, (count, count), 1
    )
    rank = jnp.sum(
        jnp.where((across == down) & earlier, 1.0, 0.0).astype(jnp.float32), axis=0, keepdims=True
    ).astype(jnp.int32)
    owner = lax.div(ids, jnp.full_like(ids, local))
    slot = (owner ^ me) * (local * capacity) + (ids - owner * local) * capacity + rank
    row = lax.broadcasted_iota(jnp.int32, (slots_total, count), 0)
    return jnp.where(row == slot, 1.0, 0.0).astype(jnp.float32).astype(jnp.bfloat16)


def stacked(refs, columns=None):
    parts = [(ref[...] if columns is None else ref[:, columns]) for ref in refs]
    if len(parts) == 1:
        return parts[0]
    return jnp.concatenate([part.astype(jnp.float32) for part in parts], axis=0).astype(jnp.bfloat16)


def dispatch(me, ids, sources, plan):
    tokens, width = sources[0].shape
    rows = plan.slots_total // plan.parts
    tile = min(2048, width)

    def body(me_ref, ids_ref, *refs):
        ins, outs, chosen = refs[: len(sources)], refs[len(sources) : -1], refs[-1]

        @pl.when(pl.program_id(0) == 0)
        def _():
            chosen[...] = selector(ids_ref[...], me_ref[0], plan.local, plan.capacity, plan.slots_total)

        block = ins[0][...]
        for other in ins[1:]:
            block = block + other[...]
        placed = jnp.dot(chosen[...], block, preferred_element_type=jnp.float32)
        for part, out in enumerate(outs):
            out[...] = placed[part * rows : (part + 1) * rows].astype(jnp.bfloat16)

    return pl.pallas_call(
        body,
        grid=(width // tile,),
        in_specs=[SMEM_SPEC, pl.BlockSpec((1, tokens), lambda i: (0, 0))]
        + [pl.BlockSpec((tokens, tile), lambda i: (0, i))] * len(sources),
        out_specs=[pl.BlockSpec((rows, tile), lambda i: (0, i))] * plan.parts,
        out_shape=[jax.ShapeDtypeStruct((rows, width), jnp.bfloat16)] * plan.parts,
        scratch_shapes=[pltpu.VMEM((plan.slots_total, tokens), jnp.bfloat16)],
        cost_estimate=cost(2 * plan.slots_total * tokens * width, (tokens + plan.slots_total) * width * 2),
        name="dispatch",
    )(me, ids, *sources)


def unpermute(me, ids, parts, plan):
    tokens = ids.shape[1]
    rows, width = parts[0].shape
    tile = min(2048, width)

    def body(me_ref, ids_ref, *refs):
        ins, out, chosen = refs[: len(parts)], refs[-2], refs[-1]

        @pl.when(pl.program_id(0) == 0)
        def _():
            chosen[...] = selector(ids_ref[...], me_ref[0], plan.local, plan.capacity, plan.slots_total)

        out[...] = lax.dot_general(
            chosen[...], stacked(ins), (((0,), (0,)), ((), ())), preferred_element_type=jnp.float32
        ).astype(jnp.bfloat16)

    return pl.pallas_call(
        body,
        grid=(width // tile,),
        in_specs=[SMEM_SPEC, pl.BlockSpec((1, tokens), lambda i: (0, 0))]
        + [pl.BlockSpec((rows, tile), lambda i: (0, i))] * len(parts),
        out_specs=pl.BlockSpec((tokens, tile), lambda i: (0, i)),
        out_shape=jax.ShapeDtypeStruct((tokens, width), jnp.bfloat16),
        scratch_shapes=[pltpu.VMEM((plan.slots_total, tokens), jnp.bfloat16)],
        cost_estimate=cost(2 * plan.slots_total * tokens * width, (tokens + plan.slots_total) * width * 2),
        name="unpermute",
    )(me, ids, *parts)


def finish(me, ids, probs, parts, arrivals, plan):
    tokens = ids.shape[1]
    rows, width = parts[0].shape
    tile = min(2048, width)

    def body(me_ref, ids_ref, probs_ref, *refs):
        ins, rest = refs[: len(parts)], refs[len(parts) :]
        others, out, chosen = rest[: len(arrivals)], rest[-2], rest[-1]

        @pl.when(pl.program_id(0) == 0)
        def _():
            chosen[...] = selector(ids_ref[...], me_ref[0], plan.local, plan.capacity, plan.slots_total)

        total = lax.dot_general(
            chosen[...], stacked(ins), (((0,), (0,)), ((), ())), preferred_element_type=jnp.float32
        )
        for other in others:
            total = total + other[...].astype(jnp.float32)
        total = total.astype(jnp.bfloat16).astype(jnp.float32)
        out[...] = (total * probs_ref[...]).astype(jnp.bfloat16)

    block = pl.BlockSpec((tokens, tile), lambda i: (0, i))
    return pl.pallas_call(
        body,
        grid=(width // tile,),
        in_specs=[
            SMEM_SPEC,
            pl.BlockSpec((1, tokens), lambda i: (0, 0)),
            pl.BlockSpec((tokens, 1), lambda i: (0, 0)),
        ]
        + [pl.BlockSpec((rows, tile), lambda i: (0, i))] * len(parts)
        + [block] * len(arrivals),
        out_specs=block,
        out_shape=jax.ShapeDtypeStruct((tokens, width), jnp.bfloat16),
        scratch_shapes=[pltpu.VMEM((plan.slots_total, tokens), jnp.bfloat16)],
        cost_estimate=cost(2 * plan.slots_total * tokens * width, (5 * tokens + plan.slots_total) * width * 2),
        name="finish",
    )(me, ids, probs, *parts, *arrivals)


def experts(parts, gate_up, down, plan):
    rows, width = parts[0].shape
    total = plan.slots_total
    wide = gate_up[0].shape[1]
    units = down[0].shape[0]
    quarter = units // plan.local
    k_tile, n_tile = min(512, width), min(1024, width)
    k_steps, n_steps = width // k_tile, width // n_tile
    count = len(parts)

    def body(*refs):
        ins = refs[:count]
        gate_refs, down_refs = refs[count : count + 2], refs[count + 2 : count + 4]
        outs = refs[count + 4 : count + 4 + 2 * count]
        acc, hidden = refs[-2], refs[-1]
        step = pl.program_id(0)

        @pl.when(step < k_steps)
        def _():
            block = stacked(ins)
            for index in range(2):
                product = jnp.dot(block, gate_refs[index][...], preferred_element_type=jnp.float32)

                @pl.when(step == 0)
                def _():
                    acc[index] = product

                @pl.when(step > 0)
                def _():
                    acc[index] = acc[index] + product

        @pl.when(step == k_steps - 1)
        def _():
            row = lax.broadcasted_iota(jnp.int32, (total, quarter), 0)
            owner = lax.div(lax.rem(row, jnp.full_like(row, plan.local * plan.capacity)), jnp.full_like(row, plan.capacity))
            for index in range(2):
                for expert in range(plan.local):
                    first = expert * 2 * quarter
                    gate = acc[index, :, first : first + quarter]
                    up = acc[index, :, first + quarter : first + 2 * quarter]
                    value = gate / (1.0 + jnp.exp(-gate)) * up
                    hidden[index, :, expert * quarter : (expert + 1) * quarter] = jnp.where(
                        owner == expert, value, 0.0
                    ).astype(jnp.bfloat16)

        @pl.when(step >= k_steps)
        def _():
            for index in range(2):
                product = jnp.dot(hidden[index], down_refs[index][...], preferred_element_type=jnp.float32)
                for part in range(count):
                    outs[index * count + part][...] = product[part * rows : (part + 1) * rows].astype(jnp.bfloat16)

    k_index = lambda i: jnp.minimum(i, k_steps - 1)
    n_index = lambda i: jnp.maximum(i - k_steps, 0)
    outs = pl.pallas_call(
        body,
        grid=(k_steps + n_steps,),
        in_specs=[pl.BlockSpec((rows, k_tile), lambda i: (0, k_index(i)))] * count
        + [pl.BlockSpec((k_tile, wide), lambda i: (k_index(i), 0))] * 2
        + [pl.BlockSpec((units, n_tile), lambda i: (0, n_index(i)))] * 2,
        out_specs=[pl.BlockSpec((rows, n_tile), lambda i: (0, n_index(i)))] * (2 * count),
        out_shape=[jax.ShapeDtypeStruct((rows, width), jnp.bfloat16)] * (2 * count),
        scratch_shapes=[
            pltpu.VMEM((2, total, wide), jnp.float32),
            pltpu.VMEM((2, total, units), jnp.bfloat16),
        ],
        cost_estimate=cost(4 * total * width * (wide + units), (wide + units) * width * 4 + total * width * 6),
        name="experts",
    )(*parts, *gate_up, *down)
    return outs[:count], outs[count:]


class Plan:
    def __init__(self, mp_count, tok_rows, route_count, local):
        self.local = local
        self.capacity = 3 * tok_rows * route_count // (2 * local * mp_count)
        self.slots_total = mp_count * local * self.capacity
        self.mp_count = mp_count
        self.pairwise = mp_count <= 8 and (local * self.capacity) % 8 == 0
        self.parts = mp_count if self.pairwise else 1


def exchange(parts, plan):
    if plan.pairwise:
        return [parts[0]] + [
            lax.ppermute(parts[k], "mp", [(i, i ^ k) for i in range(plan.mp_count)])
            for k in range(1, plan.mp_count)
        ]
    block = parts[0].reshape(plan.mp_count, -1, parts[0].shape[1])
    block = lax.all_to_all(block, "mp", split_axis=0, concat_axis=0, tiled=True)
    return [block.reshape(parts[0].shape)]


PAIR = [(0, 1), (1, 0), (2, 3), (3, 2)]
MIDDLE = [(1, 2), (2, 1)]
FAR_IN = [(3, 1), (0, 2)]
FAR_OUT = [(1, 3), (2, 0)]
OUTWARD = [(1, 0), (2, 3)]
INWARD = [(0, 1), (3, 2)]


def shards(tokens, expert_ids, gate_probs, gate_weight, up_weight, down_weight, sign_offset):
    mp_count = lax.axis_size("mp")
    dp_count = lax.axis_size("dp")
    assert dp_count == 4 and expert_ids.shape[1] == 1
    tok_rows = tokens.shape[0]
    local, _, quarter = gate_weight.shape
    hidden_total = quarter * dp_count
    plan = Plan(mp_count, tok_rows, expert_ids.shape[1], local)
    mp_index = lax.axis_index("mp")
    me = (mp_index if plan.pairwise else mp_index * 0).astype(jnp.int32).reshape(1)
    params = jnp.stack(
        [
            mixing(sign_offset[0] * 668265261 + 12345),
            (mp_index * local).astype(jnp.int32),
            (lax.axis_index("dp") * quarter).astype(jnp.int32),
        ]
    )
    ids = expert_ids.reshape(1, tok_rows)

    def gathered(own):
        near = lax.ppermute(own, "dp", PAIR)
        middle = lax.ppermute(own, "dp", MIDDLE)
        far = lax.ppermute(own, "dp", FAR_IN)
        return (
            [own],
            [near],
            [middle, lax.ppermute(middle, "dp", OUTWARD)],
            [far, lax.ppermute(far, "dp", OUTWARD)],
        )

    id_sets = [functools.reduce(jnp.add, entry) for entry in gathered(ids)]
    token_sets = gathered(tokens)
    gate_up = perturb_gate_up(params, gate_weight, up_weight, hidden_total)
    down = perturb_down(params, down_weight, hidden_total)

    returned = []
    for batch_ids, sources in zip(id_sets, token_sets):
        arrived = exchange(dispatch(me, batch_ids, sources, plan), plan)
        returned.append([exchange(parts, plan) for parts in experts(arrived, gate_up, down, plan)])

    outputs = []
    for index in range(2):
        own, near, middle, far = [entry[index] for entry in returned]
        near = lax.ppermute(unpermute(me, id_sets[1], near, plan), "dp", PAIR)
        middle = unpermute(me, id_sets[2], middle, plan)
        middle = lax.ppermute(middle + lax.ppermute(middle, "dp", INWARD), "dp", MIDDLE)
        far = unpermute(me, id_sets[3], far, plan)
        far = lax.ppermute(far + lax.ppermute(far, "dp", INWARD), "dp", FAR_OUT)
        outputs.append(finish(me, ids, gate_probs, own, [near, middle, far], plan))
    return tuple(outputs)


def solution(mesh):
    in_specs = (
        P(("dp", "mp"), None),
        P(("dp", "mp"), None),
        P(("dp", "mp"), None),
        P("mp", None, "dp"),
        P("mp", None, "dp"),
        P("mp", "dp", None),
        P(),
    )
    out_specs = (P(("dp", "mp"), None), P(("dp", "mp"), None))
    return jax.shard_map(shards, mesh=mesh, in_specs=in_specs, out_specs=out_specs, check_vma=False)
```

```python
import functools

import jax
import jax.numpy as jnp
from jax import lax
from jax.experimental import pallas as pl
from jax.experimental.pallas import tpu as pltpu
from jax.sharding import PartitionSpec as P


EPSILON = 0.005
PAIRWISE_LIMIT = 8
ID_ROWS = 8
MULTIPLIER = 73244475


def logical_right(number, amount):
    return lax.shift_right_logical(number, jnp.full_like(number, amount))


def mixing(number):
    number = number ^ logical_right(number, 16)
    number = number * MULTIPLIER
    number = number ^ logical_right(number, 16)
    number = number * MULTIPLIER
    return number ^ logical_right(number, 16)


def signed_step(hashed):
    hashed = hashed ^ logical_right(hashed, 16)
    hashed = hashed * MULTIPLIER
    hashed = hashed ^ logical_right(hashed, 16)
    hashed = hashed * MULTIPLIER
    bit = (hashed ^ logical_right(hashed, 16)) & 512
    return jnp.where(bit != 0, jnp.float32(EPSILON), jnp.float32(-EPSILON))


def cost(flops, moved):
    return pl.CostEstimate(flops=int(flops), bytes_accessed=int(moved), transcendentals=0)


SMEM_SPEC = pl.BlockSpec(memory_space=pltpu.SMEM)


def perturb_gate_up(params, gate, up, expert, hidden_total, after=()):
    _, width, quarter = gate.shape
    step_rows = min(1024, width)

    def body(params_ref, gate_ref, up_ref, *refs):
        plus_ref, minus_ref, lin_ref = refs[len(after) :]
        step = pl.program_id(0)

        @pl.when(step == 0)
        def _():
            row = lax.broadcasted_iota(jnp.int32, lin_ref.shape, 0)
            col = lax.broadcasted_iota(jnp.int32, lin_ref.shape, 1)
            lin_ref[...] = (row * hidden_total + col) * 3

        first = ((params_ref[1] + expert) * width + step * step_rows) * hidden_total + params_ref[2]
        for tag, source in ((0, gate_ref), (1, up_ref)):
            delta = signed_step((lin_ref[...] + (first * 3 + tag)) ^ params_ref[0])
            weight = source[0].astype(jnp.float32)
            columns = pl.ds(tag * quarter, quarter)
            plus_ref[:, columns] = (weight + delta).astype(jnp.bfloat16)
            minus_ref[:, columns] = (weight - delta).astype(jnp.bfloat16)

    shape = jax.ShapeDtypeStruct((width, 2 * quarter), jnp.bfloat16)
    out_spec = pl.BlockSpec((step_rows, 2 * quarter), lambda i: (i, 0))
    in_spec = pl.BlockSpec((1, step_rows, quarter), lambda i: (expert, i, 0))
    return pl.pallas_call(
        body,
        grid=(width // step_rows,),
        in_specs=[SMEM_SPEC, in_spec, in_spec] + [pl.BlockSpec(memory_space=pl.ANY)] * len(after),
        out_specs=[out_spec, out_spec],
        out_shape=[shape, shape],
        scratch_shapes=[pltpu.VMEM((step_rows, quarter), jnp.int32)],
        cost_estimate=cost(0, width * quarter * 12),
        name="perturb_gate_up",
    )(params, gate, up, *after)


def perturb_down(params, down, hidden_total, after=()):
    local, quarter, width = down.shape
    step_rows = quarter // 2
    per_expert = quarter // step_rows

    def body(params_ref, down_ref, *refs):
        plus_ref, minus_ref, lin_ref = refs[len(after) :]
        step = pl.program_id(0)

        @pl.when(step == 0)
        def _():
            row = lax.broadcasted_iota(jnp.int32, lin_ref.shape, 0)
            col = lax.broadcasted_iota(jnp.int32, lin_ref.shape, 1)
            lin_ref[...] = (row * width + col) * 3

        expert = step // per_expert
        first = (params_ref[1] + expert) * hidden_total + params_ref[2] + (step % per_expert) * step_rows
        delta = signed_step((lin_ref[...] + (first * width * 3 + 2)) ^ params_ref[0])
        weight = down_ref[...].astype(jnp.float32)
        plus_ref[...] = (weight + delta).astype(jnp.bfloat16)
        minus_ref[...] = (weight - delta).astype(jnp.bfloat16)

    shape = jax.ShapeDtypeStruct((local * quarter, width), jnp.bfloat16)
    spec = pl.BlockSpec((step_rows, width), lambda i: (i, 0))
    return pl.pallas_call(
        body,
        grid=(local * per_expert,),
        in_specs=[SMEM_SPEC, spec] + [pl.BlockSpec(memory_space=pl.ANY)] * len(after),
        out_specs=[spec, spec],
        out_shape=[shape, shape],
        scratch_shapes=[pltpu.VMEM((step_rows, width), jnp.int32)],
        cost_estimate=cost(0, down.size * 6),
        name="perturb_down",
    )(params, down.reshape(local * quarter, width), *after)


def selector(ids, me, local, capacity, slots_total):
    count = ids.shape[1]
    across = jnp.broadcast_to(ids, (count, count))
    down = jnp.transpose(across.astype(jnp.float32)).astype(jnp.int32)
    earlier = lax.broadcasted_iota(jnp.int32, (count, count), 0) < lax.broadcasted_iota(
        jnp.int32, (count, count), 1
    )
    rank = jnp.sum(
        jnp.where((across == down) & earlier, 1.0, 0.0).astype(jnp.float32), axis=0, keepdims=True
    ).astype(jnp.int32)
    owner = lax.div(ids, jnp.full_like(ids, local))
    slot = (owner ^ me) * (local * capacity) + (ids - owner * local) * capacity + rank
    row = lax.broadcasted_iota(jnp.int32, (slots_total, count), 0)
    return jnp.where(row == slot, 1.0, 0.0).astype(jnp.float32).astype(jnp.bfloat16)


def stacked(refs, columns=None):
    parts = [(ref[...] if columns is None else ref[:, columns]) for ref in refs]
    if len(parts) == 1:
        return parts[0]
    return jnp.concatenate([part.astype(jnp.float32) for part in parts], axis=0).astype(jnp.bfloat16)


def dispatch(me, ids, sources, plan):
    width = sources[0].shape[1]
    riding = ids is None
    tokens = sources[0].shape[0] - (ID_ROWS if riding else 0)
    rows = plan.slots_total // plan.parts
    tile = min(2048, width)

    def body(me_ref, *refs):
        if not riding:
            ids_ref, refs = refs[0], refs[1:]
        ins, outs, chosen = refs[: len(sources)], refs[len(sources) : -1], refs[-1]

        @pl.when(pl.program_id(0) == 0)
        def _():
            if riding:
                line = functools.reduce(
                    jnp.add, [ref[tokens : tokens + ID_ROWS, :tokens].astype(jnp.float32) for ref in ins]
                )
                found = line[:1].astype(jnp.int32)
                outs[-1][...] = found
            else:
                found = ids_ref[...]
            chosen[...] = selector(found, me_ref[0], plan.local, plan.capacity, plan.slots_total)

        block = functools.reduce(jnp.add, [ref[:tokens] for ref in ins])
        placed = jnp.dot(chosen[...], block, preferred_element_type=jnp.float32)
        for part in range(plan.parts):
            outs[part][...] = placed[part * rows : (part + 1) * rows].astype(jnp.bfloat16)

    id_spec = pl.BlockSpec((1, tokens), lambda i: (0, 0))
    id_shape = jax.ShapeDtypeStruct((1, tokens), jnp.int32)
    outs = pl.pallas_call(
        body,
        grid=(width // tile,),
        in_specs=[SMEM_SPEC]
        + [id_spec] * (not riding)
        + [pl.BlockSpec((sources[0].shape[0], tile), lambda i: (0, i))] * len(sources),
        out_specs=[pl.BlockSpec((rows, tile), lambda i: (0, i))] * plan.parts + [id_spec] * riding,
        out_shape=[jax.ShapeDtypeStruct((rows, width), jnp.bfloat16)] * plan.parts + [id_shape] * riding,
        scratch_shapes=[pltpu.VMEM((plan.slots_total, tokens), jnp.bfloat16)],
        cost_estimate=cost(2 * plan.slots_total * tokens * width, (tokens + plan.slots_total) * width * 2),
        name="dispatch",
    )(me, *([] if riding else [ids]), *sources)
    return outs[: plan.parts], outs[-1] if riding else ids


def unpermute(me, ids, parts, plan, after=()):
    tokens = ids.shape[1]
    rows, width = parts[0].shape
    tile = min(2048, width)

    def body(me_ref, ids_ref, *refs):
        ins, out, chosen = refs[: len(parts)], refs[-2], refs[-1]

        @pl.when(pl.program_id(0) == 0)
        def _():
            chosen[...] = selector(ids_ref[...], me_ref[0], plan.local, plan.capacity, plan.slots_total)

        out[...] = lax.dot_general(
            chosen[...], stacked(ins), (((0,), (0,)), ((), ())), preferred_element_type=jnp.float32
        ).astype(jnp.bfloat16)

    return pl.pallas_call(
        body,
        grid=(width // tile,),
        in_specs=[SMEM_SPEC, pl.BlockSpec((1, tokens), lambda i: (0, 0))]
        + [pl.BlockSpec((rows, tile), lambda i: (0, i))] * len(parts)
        + [pl.BlockSpec(memory_space=pl.ANY)] * len(after),
        out_specs=pl.BlockSpec((tokens, tile), lambda i: (0, i)),
        out_shape=jax.ShapeDtypeStruct((tokens, width), jnp.bfloat16),
        scratch_shapes=[pltpu.VMEM((plan.slots_total, tokens), jnp.bfloat16)],
        cost_estimate=cost(2 * plan.slots_total * tokens * width, (tokens + plan.slots_total) * width * 2),
        name="unpermute",
    )(me, ids, *parts, *after)


def finish(me, ids, probs, parts, arrivals, plan):
    tokens = ids.shape[1]
    rows, width = parts[0].shape
    tile = min(2048, width)

    def body(me_ref, ids_ref, probs_ref, *refs):
        ins, rest = refs[: len(parts)], refs[len(parts) :]
        others, out, chosen = rest[: len(arrivals)], rest[-2], rest[-1]

        @pl.when(pl.program_id(0) == 0)
        def _():
            chosen[...] = selector(ids_ref[...], me_ref[0], plan.local, plan.capacity, plan.slots_total)

        total = lax.dot_general(
            chosen[...], stacked(ins), (((0,), (0,)), ((), ())), preferred_element_type=jnp.float32
        )
        for other in others:
            total = total + other[...].astype(jnp.float32)
        total = total.astype(jnp.bfloat16).astype(jnp.float32)
        out[...] = (total * probs_ref[...]).astype(jnp.bfloat16)

    block = pl.BlockSpec((tokens, tile), lambda i: (0, i))
    return pl.pallas_call(
        body,
        grid=(width // tile,),
        in_specs=[
            SMEM_SPEC,
            pl.BlockSpec((1, tokens), lambda i: (0, 0)),
            pl.BlockSpec((tokens, 1), lambda i: (0, 0)),
        ]
        + [pl.BlockSpec((rows, tile), lambda i: (0, i))] * len(parts)
        + [block] * len(arrivals),
        out_specs=block,
        out_shape=jax.ShapeDtypeStruct((tokens, width), jnp.bfloat16),
        scratch_shapes=[pltpu.VMEM((plan.slots_total, tokens), jnp.bfloat16)],
        cost_estimate=cost(2 * plan.slots_total * tokens * width, (5 * tokens + plan.slots_total) * width * 2),
        name="finish",
    )(me, ids, probs, *parts, *arrivals)


def hidden_units(batches, gate_up, plan):
    rows, width = batches[0][0].shape
    total, local, count = plan.slots_total, plan.local, len(batches[0])
    many = len(batches)
    share = total // local
    quarter = gate_up[0][0].shape[1] // 2
    units = local * quarter
    k_tile = min(1024, width)
    k_steps = width // k_tile

    def body(*refs):
        ins = [refs[b * count : (b + 1) * count] for b in range(many)]
        refs = refs[many * count :]
        gate_refs = [refs[2 * expert : 2 * expert + 2] for expert in range(local)]
        hidden, acc, order = refs[2 * local :]
        step = pl.program_id(0)

        @pl.when(step == 0)
        def _():
            row = lax.broadcasted_iota(jnp.int32, (total, total), 0)
            slot = lax.broadcasted_iota(jnp.int32, (total, total), 1)
            expert = lax.div(row, jnp.full_like(row, share))
            inner = row - expert * share
            part = lax.div(inner, jnp.full_like(row, plan.capacity))
            source = inner + part * ((local - 1) * plan.capacity) + expert * plan.capacity
            order[...] = jnp.where(slot == source, 1.0, 0.0).astype(jnp.float32).astype(jnp.bfloat16)

        ordered = [
            jnp.dot(order[...], stacked(part), preferred_element_type=jnp.float32).astype(jnp.bfloat16)
            for part in ins
        ]
        for expert in range(local):
            block = jnp.concatenate([one[expert * share : (expert + 1) * share] for one in ordered], axis=0)
            columns = slice(expert * 2 * quarter, (expert + 1) * 2 * quarter)
            for index in range(2):
                product = jnp.dot(block, gate_refs[expert][index][...], preferred_element_type=jnp.float32)

                @pl.when(step == 0)
                def _():
                    acc[index, :, columns] = product

                @pl.when(step > 0)
                def _():
                    acc[index, :, columns] = acc[index, :, columns] + product

        @pl.when(step == k_steps - 1)
        def _():
            for index in range(2):
                for expert in range(local):
                    first = expert * 2 * quarter
                    for b in range(many):
                        gate = acc[index, b * share : (b + 1) * share, first : first + quarter]
                        up = acc[index, b * share : (b + 1) * share, first + quarter : first + 2 * quarter]
                        value = (gate / (1.0 + jnp.exp(-gate)) * up).astype(jnp.bfloat16)
                        hidden[index, b * total : (b + 1) * total, expert * quarter : (expert + 1) * quarter] = (
                            lax.dot_general(
                                order[expert * share : (expert + 1) * share, :],
                                value,
                                (((0,), (0,)), ((), ())),
                                preferred_element_type=jnp.float32,
                            ).astype(jnp.bfloat16)
                        )

    shape = (2, many * total, units)
    return pl.pallas_call(
        body,
        grid=(k_steps,),
        in_specs=[pl.BlockSpec((rows, k_tile), lambda i: (0, i))] * (many * count)
        + [pl.BlockSpec((k_tile, 2 * quarter), lambda i: (i, 0))] * (2 * local),
        out_specs=pl.BlockSpec(shape, lambda i: (0, 0, 0)),
        out_shape=jax.ShapeDtypeStruct(shape, jnp.bfloat16),
        scratch_shapes=[
            pltpu.VMEM((2, many * share, 2 * units), jnp.float32),
            pltpu.VMEM((total, total), jnp.bfloat16),
        ],
        cost_estimate=cost(8 * many * total * width * units, units * width * 8),
        name="hidden_units",
    )(*[part for batch in batches for part in batch], *[one for pair in gate_up for one in pair])


def down_rows(hidden, index, down, many, plan):
    total, count = plan.slots_total, plan.parts
    rows = total // count
    units, width = down.shape
    n_tile = min(1024, width)

    def body(hidden_ref, down_ref, *outs):
        product = jnp.dot(hidden_ref[0], down_ref[...], preferred_element_type=jnp.float32)
        for number, out in enumerate(outs):
            out[...] = product[number * rows : (number + 1) * rows].astype(jnp.bfloat16)

    outs = pl.pallas_call(
        body,
        grid=(width // n_tile,),
        in_specs=[
            pl.BlockSpec((1, many * total, units), lambda i: (index, 0, 0)),
            pl.BlockSpec((units, n_tile), lambda i: (0, i)),
        ],
        out_specs=[pl.BlockSpec((rows, n_tile), lambda i: (0, i))] * (many * count),
        out_shape=[jax.ShapeDtypeStruct((rows, width), jnp.bfloat16)] * (many * count),
        cost_estimate=cost(2 * many * total * width * units, units * width * 2 + many * total * width * 2),
        name="down_rows",
    )(hidden, down)
    return [outs[b * count : (b + 1) * count] for b in range(many)]


class Plan:
    def __init__(self, mp_count, tok_rows, route_count, local):
        self.local = local
        self.capacity = 3 * tok_rows * route_count // (2 * local * mp_count)
        self.slots_total = mp_count * local * self.capacity
        self.mp_count = mp_count
        self.pairwise = mp_count <= PAIRWISE_LIMIT
        assert (local * self.capacity) % 8 == 0 or not self.pairwise
        self.parts = mp_count if self.pairwise else 1


def exchange(parts, plan):
    if plan.pairwise:
        return [parts[0]] + [
            lax.ppermute(parts[k], "mp", [(i, i ^ k) for i in range(plan.mp_count)])
            for k in range(1, plan.mp_count)
        ]
    block = parts[0].reshape(plan.mp_count, -1, parts[0].shape[1])
    block = lax.all_to_all(block, "mp", split_axis=0, concat_axis=0, tiled=True)
    return [block.reshape(parts[0].shape)]


def move(value, pairs):
    return lax.ppermute(value, "dp", pairs)


PAIR = [(0, 1), (1, 0), (2, 3), (3, 2)]
MIDDLE = [(1, 2), (2, 1)]
FAR_OUT = [(1, 3), (2, 0)]
OUTWARD = [(1, 0), (2, 3)]
INWARD = [(0, 1), (3, 2)]


def shards(tokens, expert_ids, gate_probs, gate_weight, up_weight, down_weight, sign_offset):
    mp_count = lax.axis_size("mp")
    dp_count = lax.axis_size("dp")
    assert dp_count == 4 and expert_ids.shape[1] == 1
    tok_rows = tokens.shape[0]
    local, _, quarter = gate_weight.shape
    hidden_total = quarter * dp_count
    plan = Plan(mp_count, tok_rows, expert_ids.shape[1], local)
    mp_index, dp_index = lax.axis_index("mp"), lax.axis_index("dp")
    me = (mp_index if plan.pairwise else mp_index * 0).astype(jnp.int32).reshape(1)
    params = jnp.stack(
        [
            mixing(sign_offset[0] * 668265261 + 12345),
            (mp_index * local).astype(jnp.int32),
            (dp_index * quarter).astype(jnp.int32),
        ]
    )
    ids = expert_ids.reshape(1, tok_rows)

    assert local * mp_count <= 256 and tok_rows <= tokens.shape[1]
    line = jnp.pad(ids.astype(jnp.bfloat16), ((0, ID_ROWS - 1), (0, tokens.shape[1] - tok_rows)))
    package = jnp.concatenate([tokens, line], axis=0)
    near = move(package, PAIR)
    middle = move(package, MIDDLE)
    middle_edge = move(middle, OUTWARD)
    far = move(near, MIDDLE)
    far_edge = move(far, OUTWARD)

    down = perturb_down(params, down_weight, hidden_total)
    gate_up = [perturb_gate_up(params, gate_weight, up_weight, expert, hidden_total) for expert in range(local)]
    arrived, found = {}, {}
    for label, batch_ids, sources in (
        ("own", ids, [tokens]),
        ("near", None, [near]),
        ("mid", None, [middle, middle_edge]),
        ("far", None, [far, far_edge]),
    ):
        sent, found[label] = dispatch(me, batch_ids, sources, plan)
        arrived[label] = exchange(sent, plan)
    hidden = [
        hidden_units([arrived["own"], arrived["near"]], gate_up, plan),
        hidden_units([arrived["mid"], arrived["far"]], gate_up, plan),
    ]
    own, near = zip(*[down_rows(hidden[0], i, down[i], 2, plan) for i in range(2)])
    middle, far = zip(*[down_rows(hidden[1], i, down[i], 2, plan) for i in range(2)])

    outputs = []
    for i in range(2):
        near_part = unpermute(me, found["near"], exchange(near[i], plan), plan)
        near_part = move(near_part, PAIR)
        far_part = unpermute(me, found["far"], exchange(far[i], plan), plan)
        far_part = move(far_part + move(far_part, INWARD), FAR_OUT)
        mid_part = unpermute(me, found["mid"], exchange(middle[i], plan), plan)
        mid_part = move(mid_part + move(mid_part, INWARD), MIDDLE)
        own_parts = exchange(own[i], plan)
        outputs.append(finish(me, ids, gate_probs, own_parts, [near_part, mid_part, far_part], plan))
    return tuple(outputs)


def solution(mesh):
    in_specs = (
        P(("dp", "mp"), None),
        P(("dp", "mp"), None),
        P(("dp", "mp"), None),
        P("mp", None, "dp"),
        P("mp", None, "dp"),
        P("mp", "dp", None),
        P(),
    )
    out_specs = (P(("dp", "mp"), None), P(("dp", "mp"), None))
    return jax.shard_map(shards, mesh=mesh, in_specs=in_specs, out_specs=out_specs, check_vma=False)
```
